32 devices in a mesh: tm: 8 (over z, y), pix: 4 (over x, core).
Axes of the slice: x: 2, y: 2, z: 4, core: 2. Of those that a mesh axis runs over, the one named last changes fastest.
Arguments:
- counts: float32 [1024, 16384], P('tm', 'pix'), may hold values from 0.5 to 15
- dead_time: float32 [16384], P('pix'), may hold values from 0.002 to 0.03
- flat_field: float32 [16384], P('pix'), may hold values from 0.3 to 3
- cycle_map: int32 [16384], P('pix'), may hold values from 0 to 31, as said below
Outputs:
- two_time: float32 [32, 1024, 1024], P('pix', 'tm')
The draws below stay inside these ranges and needn't reach their ends.
Inputs may be any that keep to these rules, and one draw needn't show every extreme that they name: `cycle_map`: every cycle holds at least one pixel.
All inputs are finite; a program needn't handle non-finite values.
Results may differ from the reference program's by a relative error of at most 0.00042.
Values may be sent and summed in bfloat16 or wider, within the bound.
A program may use at most 64 MiB of HBM per device.

```python
import math
import jax
import jax.numpy as jnp
from jax import lax

FRAMES = 1024
CYCLES = 32
PIXELS = 16384


def draw_cycle_map(key, part):
    first_key = jax.random.fold_in(key, 11)
    second_key = jax.random.fold_in(key, 23)
    uniform_ints = jax.random.randint(first_key, (PIXELS,), 0, CYCLES * CYCLES)
    bounds = jnp.arange(1, CYCLES, dtype=jnp.int32) ** 2
    cycles = jnp.sum((uniform_ints[:, None] >= bounds[None, :]).astype(jnp.int32), axis=1).astype(jnp.int32)
    chosen = jax.random.permutation(second_key, PIXELS)[:CYCLES]
    return cycles.at[chosen].set(jnp.arange(CYCLES, dtype=jnp.int32))


def level_of(own_key, extent, cuts, smallest, high):
    def one(axis_at, blocks):
        draws = jax.random.uniform(jax.random.fold_in(jax.random.fold_in(own_key, 6), axis_at), (blocks,), jnp.float32, smallest / len(cuts), high / len(cuts))
        return jnp.repeat(jnp.exp(draws), extent[axis_at] // blocks).reshape((-1,) + (1,) * (len(extent) - axis_at - 1))

    level = one(*cuts[0])
    for cut in cuts[1:]:
        level = level * one(*cut)
    return level


def setup_inputs(seed: int = 0) -> dict:
    streams_of = jax.random.split(jax.random.key(seed), 5)
    counts = jnp.clip(jnp.exp(math.log(15.0) - 3.4011974 * jax.random.uniform(streams_of[0], (FRAMES, PIXELS), jnp.float32) ** level_of(streams_of[0], (FRAMES, PIXELS), ((0, 8), (1, 4)), -0.2, 0.2)), 0.5, 15.0)
    dead_time = jnp.clip(jnp.exp(math.log(0.03) - 2.70805 * jax.random.uniform(streams_of[1], (PIXELS,), jnp.float32) ** level_of(streams_of[1], (PIXELS,), ((0, 4),), -0.2, 0.2)), 0.002, 0.03)
    flat_field = jnp.clip(jnp.exp(math.log(3.0) - 2.3025851 * jax.random.uniform(streams_of[2], (PIXELS,), jnp.float32) ** level_of(streams_of[2], (PIXELS,), ((0, 4),), -0.2, 0.2)), 0.3, 3.0)
    cycle_map = draw_cycle_map(jax.random.fold_in(streams_of[4], 71), 0)
    return dict(counts=counts, dead_time=dead_time, flat_field=flat_field, cycle_map=cycle_map)


def reference(counts, dead_time, flat_field, cycle_map):
    photons = counts.astype(jnp.float32)
    intensity = (photons / (1.0 - dead_time[None, :] * photons) * flat_field[None, :]).astype(jnp.bfloat16)
    widened = intensity.astype(jnp.float32)
    cycle_onehot = (cycle_map[None, :] == jnp.arange(CYCLES, dtype=jnp.int32)[:, None]).astype(jnp.float32)
    cycle_size = jnp.sum(cycle_onehot, axis=1)
    cycle_sum = jnp.dot(cycle_onehot, widened.T, precision=lax.Precision.HIGHEST)

    def one_cycle(weights):
        masked = widened * weights[None, :]
        return jnp.dot(masked, widened.T, precision=lax.Precision.HIGHEST)

    gram = lax.map(one_cycle, cycle_onehot)
    return cycle_size[:, None, None] * gram / (cycle_sum[:, :, None] * cycle_sum[:, None, :])
```

```python
import jax
import jax.numpy as jnp
from jax import lax
from jax.sharding import PartitionSpec as P

CYCLES = 32


def inner_extent(count):
    return max(d for d in range(1, count + 1) if count % d == 0 and d * d <= count)


def per_device(counts, dead_time, flat_field, cycle_map):
    intensity = (counts / (1.0 - dead_time[None, :] * counts) * flat_field[None, :]).astype(
        jnp.bfloat16
    )
    frames, pixels = intensity.shape
    tm, pix = lax.axis_size("tm"), lax.axis_size("pix")
    inner = inner_extent(tm)
    outer = tm // inner
    cores = 2 if pix % 2 == 0 else 1
    across = pix // cores
    owned = CYCLES // pix
    at_tm, at_pix = lax.axis_index("tm"), lax.axis_index("pix")
    z, y = at_tm // inner, at_tm % inner
    x, core = at_pix // cores, at_pix % cores

    def shift_z(value, k=1):
        return lax.ppermute(
            value, "tm", [(i, (i // inner + k) % outer * inner + i % inner) for i in range(tm)]
        )

    def shift_y(value, k):
        return lax.ppermute(
            value, "tm", [(i, i // inner * inner + (i % inner + k) % inner) for i in range(tm)]
        )

    def shift_x(value, k):
        return lax.ppermute(
            value, "pix", [(i, (i // cores + k) % across * cores + i % cores) for i in range(pix)]
        )

    def swap_core(value):
        return lax.ppermute(
            value, "pix", [(i, i // cores * cores + (i % cores + 1) % cores) for i in range(pix)]
        )

    own = [intensity]
    for s in range(1, outer):
        own.append(shift_z(own[-1]))
    blocks = {}
    for s in range(outer):
        blocks[s, 0] = own[s]
        for k in range(1, inner):
            if s == outer - 1 and s > 0:
                half = frames // 2
                blocks[s, k] = jnp.concatenate(
                    [shift_y(own[s][:half], k), shift_z(blocks[s - 1, k][half:])], axis=0
                )
            else:
                blocks[s, k] = shift_y(own[s], k)

    def cycles_of(owner_x, owner_core):
        first = (owner_x * cores + owner_core) * owned
        return first + jnp.arange(owned, dtype=jnp.int32)

    def onehot_of(owner_core):
        ids = jnp.concatenate([cycles_of((x + k) % across, owner_core) for k in range(across)])
        return (cycle_map[None, :] == ids[:, None]).astype(jnp.bfloat16)

    mine = onehot_of(core)
    theirs = onehot_of((core + 1) % cores)

    def dot(left, right):
        return lax.dot_general(
            left, right, (((1,), (1,)), ((), ())), preferred_element_type=jnp.float32
        )

    def reduce_owned(to_theirs, to_mine):
        if cores > 1:
            to_mine = to_mine + swap_core(to_theirs())
        total = to_mine[:owned]
        for k in range(1, across):
            total = total + shift_x(to_mine[k * owned : (k + 1) * owned], k)
        return total

    def small(onehot):
        sums = dot(onehot, intensity)
        sizes = jnp.sum(onehot.astype(jnp.float32), axis=1, keepdims=True)
        return jnp.concatenate([sums, jnp.broadcast_to(sizes, sums.shape)], axis=1)

    totals = reduce_owned(lambda: small(theirs), small(mine))
    row_sums, sizes = totals[:, :frames], totals[:, frames]
    sum_ring = [row_sums]
    for s in range(1, outer):
        sum_ring.append(shift_z(sum_ring[-1]))
    sum_ring = jnp.stack(sum_ring)
    column_sums = [sum_ring] + [shift_y(sum_ring, k) for k in range(1, inner)]

    def gram(onehot, block):
        masked = (onehot[:, None, :] * intensity[None, :, :]).reshape(-1, pixels)
        return dot(masked, block).reshape(onehot.shape[0], frames, frames)

    out = jnp.zeros((owned, frames, tm * frames), jnp.float32)
    order = sorted(blocks, key=lambda at: at[0] + at[1])
    for s, k in order:
        block = blocks[s, k]
        total = reduce_owned(lambda: gram(theirs, block), gram(mine, block))
        column = column_sums[k][s]
        value = sizes[:, None, None] * total / (row_sums[:, :, None] * column[:, None, :])
        at = ((z - s) % outer * inner + (y - k) % inner) * frames
        out = lax.dynamic_update_slice_in_dim(out, value, at, 2)
    return out


def solution(mesh):
    placed = (P("tm", "pix"), P("pix"), P("pix"), P("pix"))
    return jax.shard_map(
        per_device, mesh=mesh, in_specs=placed, out_specs=P("pix", "tm", None), check_vma=False
    )
```

```python
import jax
import jax.numpy as jnp
from jax import lax
from jax.sharding import PartitionSpec as P

CYCLES = 32


def inner_extent(count):
    return max(d for d in range(1, count + 1) if count % d == 0 and d * d <= count)


def per_device(counts, dead_time, flat_field, cycle_map):
    intensity = (counts / (1.0 - dead_time[None, :] * counts) * flat_field[None, :]).astype(
        jnp.bfloat16
    )
    frames, pixels = intensity.shape
    tm, pix = lax.axis_size("tm"), lax.axis_size("pix")
    inner = inner_extent(tm)
    outer = tm // inner
    cores = 2 if pix % 2 == 0 else 1
    across = pix // cores
    owned = CYCLES // pix
    at_tm, at_pix = lax.axis_index("tm"), lax.axis_index("pix")
    z, y = at_tm // inner, at_tm % inner
    x, core = at_pix // cores, at_pix % cores

    def shift_z(value, k=1):
        return lax.ppermute(
            value, "tm", [(i, (i // inner + k) % outer * inner + i % inner) for i in range(tm)]
        )

    def shift_y(value, k):
        return lax.ppermute(
            value, "tm", [(i, i // inner * inner + (i % inner + k) % inner) for i in range(tm)]
        )

    def shift_x(value, k):
        return lax.ppermute(
            value, "pix", [(i, (i // cores + k) % across * cores + i % cores) for i in range(pix)]
        )

    def swap_core(value):
        return lax.ppermute(
            value, "pix", [(i, i // cores * cores + (i % cores + 1) % cores) for i in range(pix)]
        )

    blocks = {(0, 0): intensity}
    for s in range(outer):
        if s > 0:
            blocks[s, 0] = shift_z(blocks[s - 1, 0])
        for k in range(1, inner):
            if s == outer - 1 and s > 0:
                half = frames // 2
                first = shift_y(blocks[s, 0][:half], k)
                second = shift_z(blocks[s - 1, k][half:])
                blocks[s, k] = jnp.concatenate([first, second], axis=0)
            else:
                blocks[s, k] = shift_y(blocks[s, 0], k)

    def onehot_of(owner_core):
        ids = jnp.concatenate(
            [
                ((x + k) % across * cores + owner_core) * owned
                + jnp.arange(owned, dtype=jnp.int32)
                for k in range(across)
            ]
        )
        return (cycle_map[None, :] == ids[:, None]).astype(jnp.bfloat16)

    mine = onehot_of(core)
    theirs = onehot_of((core + 1) % cores)
    extended = jnp.concatenate([intensity, jnp.ones((8, pixels), jnp.bfloat16)], axis=0)
    rows = frames + 8

    def gram(onehot, right):
        masked = (onehot[:, None, :] * extended[None, :, :]).reshape(-1, pixels)
        return lax.dot_general(
            masked, right, (((1,), (1,)), ((), ())), preferred_element_type=jnp.float32
        ).reshape(onehot.shape[0], rows, right.shape[0])

    def reduce_owned(right):
        if cores > 1:
            away = gram(theirs, right)
            away = swap_core(away)
        here = gram(mine, right)
        if cores > 1:
            here = here + away
        total = here[:owned]
        for k in range(1, across):
            total = total + shift_x(here[k * owned : (k + 1) * owned], k)
        return total

    groups = [[(0, 0)]]
    for s in range(outer):
        later = [(s, k) for k in range(1, inner)]
        if s + 1 < outer:
            later.append((s + 1, 0))
        if later:
            groups.append(later)

    out = jnp.zeros((owned, frames, tm * frames), jnp.float32)
    for g, members in enumerate(groups):
        if g == 0:
            total = reduce_owned(extended)
            row_sums = total[:, :frames, frames]
            scale = total[:, frames, frames][:, None, None] / row_sums[:, :, None]
        else:
            total = reduce_owned(jnp.concatenate([blocks[at] for at in members], axis=0))
        for i, (s, k) in enumerate(members):
            part = total[:, :, i * frames : (i + 1) * frames]
            value = part[:, :frames] * scale / part[:, frames : frames + 1]
            at = ((z - s) % outer * inner + (y - k) % inner) * frames
            out = lax.dynamic_update_slice_in_dim(out, value, at, 2)
    return out


def solution(mesh):
    placed = (P("tm", "pix"), P("pix"), P("pix"), P("pix"))

    return jax.shard_map(
        per_device, mesh=mesh, in_specs=placed, out_specs=P("pix", "tm", None), check_vma=False
    )
```

```python
import jax
import jax.numpy as jnp
from jax import lax
from jax.experimental import pallas as pl
from jax.experimental.pallas import tpu as pltpu
from jax.sharding import PartitionSpec as P

CYCLES = 32
CENTRE = 3.62
STEPS = 3500.0


def inner_extent(count):
    return max(d for d in range(1, count + 1) if count % d == 0 and d * d <= count)


def encode(here, count, first, owned):
    _, rows, columns = here.shape

    def kernel(count_ref, here_ref, sent_ref):
        inverse = 1.0 / jnp.maximum(count_ref[first + pl.program_id(0)], jnp.full((1, columns), 1.0))
        level = jnp.log2(jnp.maximum(here_ref[0] * inverse, 0.02)) - CENTRE
        sent_ref[0] = jnp.round(level * STEPS).astype(jnp.int32).astype(jnp.int16)

    return pl.pallas_call(
        kernel,
        grid_spec=pltpu.PrefetchScalarGridSpec(
            num_scalar_prefetch=1,
            grid=(owned,),
            in_specs=[pl.BlockSpec((1, rows, columns), lambda r, c: (first + r, 0, 0))],
            out_specs=pl.BlockSpec((1, rows, columns), lambda r, c: (r, 0, 0)),
        ),
        out_shape=jax.ShapeDtypeStruct((owned, rows, columns), jnp.int16),
        cost_estimate=pl.CostEstimate(flops=owned * rows * columns, bytes_accessed=here.size * 4, transcendentals=0),
    )(count, here)


def finish(here, gots, counts, scale, places, out, frames):
    _, rows, columns = here.shape
    owned = scale.shape[0]
    parts = columns // frames

    def kernel(place_ref, count_ref, here_ref, *refs):
        got_refs, scale_ref, out_ref = refs[: len(gots)], refs[-3], refs[-1]
        total = here_ref[0]
        for k, got_ref in enumerate(got_refs):
            level = got_ref[0].astype(jnp.int32).astype(jnp.float32) * (1.0 / STEPS) + CENTRE
            total = total + jnp.exp2(level) * count_ref[k * owned + pl.program_id(1)]
        out_ref[0] = total[:frames] * scale_ref[0] / total[frames : frames + 1]

    block = pl.BlockSpec((1, rows, frames), lambda i, r, p, c: (r, 0, i))
    return pl.pallas_call(
        kernel,
        grid_spec=pltpu.PrefetchScalarGridSpec(
            num_scalar_prefetch=2,
            grid=(parts, owned),
            in_specs=[block] * (1 + len(gots))
            + [
                pl.BlockSpec((1, frames, 1), lambda i, r, p, c: (r, 0, 0)),
                pl.BlockSpec(memory_space=pl.ANY),
            ],
            out_specs=pl.BlockSpec((1, frames, frames), lambda i, r, p, c: (r, 0, p[i])),
        ),
        out_shape=jax.ShapeDtypeStruct(out.shape, out.dtype),
        input_output_aliases={4 + len(gots): 0},
        cost_estimate=pl.CostEstimate(flops=owned * rows * columns, bytes_accessed=here.size * 4, transcendentals=0),
    )(places, counts, here, *gots, scale, out)


def per_device(counts, dead_time, flat_field, cycle_map):
    intensity = (counts / (1.0 - dead_time[None, :] * counts) * flat_field[None, :]).astype(
        jnp.bfloat16
    )
    frames, pixels = intensity.shape
    tm, pix = lax.axis_size("tm"), lax.axis_size("pix")
    inner = inner_extent(tm)
    outer = tm // inner
    cores = 2 if pix % 2 == 0 else 1
    across = pix // cores
    owned = CYCLES // pix
    at_tm, at_pix = lax.axis_index("tm"), lax.axis_index("pix")
    z, y = at_tm // inner, at_tm % inner
    x, core = at_pix // cores, at_pix % cores

    def shift_z(value, k=1):
        return lax.ppermute(
            value, "tm", [(i, (i // inner + k) % outer * inner + i % inner) for i in range(tm)]
        )

    def shift_y(value, k):
        return lax.ppermute(
            value, "tm", [(i, i // inner * inner + (i % inner + k) % inner) for i in range(tm)]
        )

    def shift_x(value, k):
        return lax.ppermute(
            value, "pix", [(i, (i // cores + k) % across * cores + i % cores) for i in range(pix)]
        )

    def swap_core(value):
        return lax.ppermute(
            value, "pix", [(i, i // cores * cores + (i % cores + 1) % cores) for i in range(pix)]
        )

    blocks = {(0, 0): intensity}
    for s in range(outer):
        if s > 0:
            blocks[s, 0] = shift_z(blocks[s - 1, 0])
        for k in range(1, inner):
            if s == outer - 1 and s > 0:
                half = frames // 2
                first = shift_y(blocks[s, 0][:half], k)
                second = shift_z(blocks[s - 1, k][half:])
                blocks[s, k] = jnp.concatenate([first, second], axis=0)
            else:
                blocks[s, k] = shift_y(blocks[s, 0], k)

    def onehot_of(owner_core):
        ids = jnp.concatenate(
            [
                ((x + k) % across * cores + owner_core) * owned
                + jnp.arange(owned, dtype=jnp.int32)
                for k in range(across)
            ]
        )
        return (cycle_map[None, :] == ids[:, None]).astype(jnp.bfloat16)

    mine = onehot_of(core)
    theirs = onehot_of((core + 1) % cores)
    extended = jnp.concatenate([intensity, jnp.ones((8, pixels), jnp.bfloat16)], axis=0)
    rows = frames + 8

    def gram(onehot, right):
        masked = (onehot[:, None, :] * extended[None, :, :]).reshape(-1, pixels)
        return lax.dot_general(
            masked, right, (((1,), (1,)), ((), ())), preferred_element_type=jnp.float32
        ).reshape(onehot.shape[0], rows, right.shape[0])

    def reduce_core(right):
        if cores > 1:
            away = gram(theirs, right)
            away = swap_core(away)
        here = gram(mine, right)
        return here + away if cores > 1 else here

    groups = [[(0, 0)]]
    for s in range(outer):
        later = [(s, k) for k in range(1, inner)]
        if s + 1 < outer:
            later.append((s + 1, 0))
        if later:
            groups.append(later)

    out = jnp.zeros((owned, frames, tm * frames), jnp.float32)
    for g, members in enumerate(groups):
        right = extended if g == 0 else jnp.concatenate([blocks[at] for at in members], axis=0)
        here = reduce_core(right)
        if g == 0:
            sent_count = here[:, frames, frames]
            total, got_count = here[:owned], []
            for k in range(1, across):
                got = shift_x(here[k * owned : (k + 1) * owned], k)
                got_count.append(got[:, frames, frames])
                total = total + got
            got_count = jnp.concatenate(got_count) if got_count else jnp.zeros((1,), jnp.float32)
            scale = total[:, frames : frames + 1, frames : frames + 1] / total[:, :frames, frames : frames + 1]
            value = total[:, :frames, :frames] * scale / total[:, frames : frames + 1, :frames]
            out = lax.dynamic_update_slice_in_dim(out, value, at_tm * frames, 2)
            continue
        gots = []
        for k in range(1, across):
            sent = encode(here, sent_count, k * owned, owned)
            gots.append(shift_x(sent, k))
        if frames % 128:
            total = here[:owned]
            for k, got in enumerate(gots):
                level = got.astype(jnp.float32) * (1.0 / STEPS) + CENTRE
                total = total + jnp.exp2(level) * got_count[k * owned : (k + 1) * owned, None, None]
            value = total[:, :frames] * scale / total[:, frames : frames + 1]
            for i, (s, k) in enumerate(members):
                at = ((z - s) % outer * inner + (y - k) % inner) * frames
                part = value[:, :, i * frames : (i + 1) * frames]
                out = lax.dynamic_update_slice_in_dim(out, part, at, 2)
            continue
        places = jnp.stack(
            [(z - s) % outer * inner + (y - k) % inner for s, k in members]
        ).astype(jnp.int32)
        out = finish(here, gots, got_count, scale, places, out, frames)
    return out


def solution(mesh):
    placed = (P("tm", "pix"), P("pix"), P("pix"), P("pix"))

    return jax.shard_map(
        per_device, mesh=mesh, in_specs=placed, out_specs=P("pix", "tm", None), check_vma=False
    )
```

```python
import math

import jax
import jax.numpy as jnp
from jax import lax
from jax.sharding import PartitionSpec as P

CYCLES = 32


def inner_extent(count):
    return max(d for d in range(1, count + 1) if count % d == 0 and d * d <= count)


def per_device(counts, dead_time, flat_field, cycle_map):
    intensity = (counts / (1.0 - dead_time[None, :] * counts) * flat_field[None, :]).astype(
        jnp.bfloat16
    )
    frames, pixels = intensity.shape
    tm, pix = lax.axis_size("tm"), lax.axis_size("pix")
    inner = inner_extent(tm)
    outer = tm // inner
    cores = 2 if pix % 2 == 0 else 1
    across = pix // cores
    owned = CYCLES // pix
    at_tm, at_pix = lax.axis_index("tm"), lax.axis_index("pix")
    z, y = at_tm // inner, at_tm % inner
    x, core = at_pix // cores, at_pix % cores

    def shift_z(value, k=1):
        return lax.ppermute(
            value, "tm", [(i, (i // inner + k) % outer * inner + i % inner) for i in range(tm)]
        )

    def shift_y(value, k):
        return lax.ppermute(
            value, "tm", [(i, i // inner * inner + (i % inner + k) % inner) for i in range(tm)]
        )

    def shift_x(value, k):
        return lax.ppermute(
            value, "pix", [(i, (i // cores + k) % across * cores + i % cores) for i in range(pix)]
        )

    def swap_core(value):
        return lax.ppermute(
            value, "pix", [(i, i // cores * cores + (i % cores + 1) % cores) for i in range(pix)]
        )

    blocks = {(0, 0): intensity}
    for s in range(outer):
        if s > 0:
            blocks[s, 0] = shift_z(blocks[s - 1, 0])
        for k in range(1, inner):
            if s == outer - 1 and s > 0:
                half = frames // 2
                first = shift_y(blocks[s, 0][:half], k)
                second = shift_z(blocks[s - 1, k][half:])
                blocks[s, k] = jnp.concatenate([first, second], axis=0)
            else:
                blocks[s, k] = shift_y(blocks[s, 0], k)

    def onehot_of(owner_core):
        ids = jnp.concatenate(
            [
                ((x + k) % across * cores + owner_core) * owned
                + jnp.arange(owned, dtype=jnp.int32)
                for k in range(across)
            ]
        )
        return (cycle_map[None, :] == ids[:, None]).astype(jnp.bfloat16)

    onehots = jnp.concatenate([onehot_of((core + c) % cores) for c in range(cores)])
    kept = owned * across
    extended = jnp.concatenate([intensity, jnp.ones((8, pixels), jnp.bfloat16)], axis=0)
    rows = frames + 8

    def gram(onehot, right):
        masked = (onehot[:, None, :] * extended[None, :, :]).reshape(-1, pixels)
        return lax.dot_general(
            masked, right, (((1,), (1,)), ((), ())), preferred_element_type=jnp.float32
        ).reshape(onehot.shape[0], rows, right.shape[0])

    low, high = math.log2(0.0218), math.log2(6800.0 * pixels * cores)
    centre, steps = (high + low) / 2, 65400 / (high - low)
    zero = -32700 + 32

    def reduce_owned(g, right):
        here = gram(onehots, right)
        if cores > 1:
            away = swap_core(here[kept:])
            here = here[:kept] + away
        total = here[:owned]
        for k in range(1, across):
            sent = here[k * owned : (k + 1) * owned]
            if g > 0:
                level = (jnp.log2(jnp.maximum(sent, 0.0218)) - centre) * steps
                sent = jnp.round(level).astype(jnp.int16)
            got = shift_x(sent, k)
            if g > 0:
                level = got.astype(jnp.float32)
                got = jnp.where(level > zero, jnp.exp2(level * (1.0 / steps) + centre), 0.0)
            total = total + got
        return total

    groups = [[(0, 0)]]
    for s in range(outer):
        later = [(s, k) for k in range(1, inner)]
        if s + 1 < outer:
            later.append((s + 1, 0))
        if later:
            groups.append(later)

    out = jnp.zeros((owned, frames, tm * frames), jnp.float32)
    for g, members in enumerate(groups):
        if g == 0:
            total = reduce_owned(0, extended)
            row_sums = total[:, :frames, frames]
            scale = total[:, frames, frames][:, None, None] / row_sums[:, :, None]
        else:
            total = reduce_owned(g, jnp.concatenate([blocks[at] for at in members], axis=0))
        for i, (s, k) in enumerate(members):
            part = total[:, :, i * frames : (i + 1) * frames]
            value = part[:, :frames] * scale / part[:, frames : frames + 1]
            at = ((z - s) % outer * inner + (y - k) % inner) * frames
            out = lax.dynamic_update_slice_in_dim(out, value, at, 2)
    return out


def solution(mesh):
    placed = (P("tm", "pix"), P("pix"), P("pix"), P("pix"))

    return jax.shard_map(
        per_device, mesh=mesh, in_specs=placed, out_specs=P("pix", "tm", None), check_vma=False
    )
```

```python
import math

import jax
import jax.numpy as jnp
from jax import lax
from jax.sharding import PartitionSpec as P

CYCLES = 32


def inner_extent(count):
    return max(d for d in range(1, count + 1) if count % d == 0 and d * d <= count)


def per_device(counts, dead_time, flat_field, cycle_map):
    intensity = (counts / (1.0 - dead_time[None, :] * counts) * flat_field[None, :]).astype(
        jnp.bfloat16
    )
    frames, pixels = intensity.shape
    tm, pix = lax.axis_size("tm"), lax.axis_size("pix")
    inner = inner_extent(tm)
    outer = tm // inner
    cores = 2 if pix % 2 == 0 else 1
    across = pix // cores
    owned = CYCLES // pix
    at_tm, at_pix = lax.axis_index("tm"), lax.axis_index("pix")
    z, y = at_tm // inner, at_tm % inner
    x, core = at_pix // cores, at_pix % cores

    def shift_z(value, k=1):
        return lax.ppermute(
            value, "tm", [(i, (i // inner + k) % outer * inner + i % inner) for i in range(tm)]
        )

    def shift_y(value, k):
        return lax.ppermute(
            value, "tm", [(i, i // inner * inner + (i % inner + k) % inner) for i in range(tm)]
        )

    def shift_x(value, k):
        return lax.ppermute(
            value, "pix", [(i, (i // cores + k) % across * cores + i % cores) for i in range(pix)]
        )

    def swap_core(value):
        return lax.ppermute(
            value, "pix", [(i, i // cores * cores + (i % cores + 1) % cores) for i in range(pix)]
        )

    blocks = {(0, 0): intensity}
    for s in range(outer):
        if s > 0:
            blocks[s, 0] = shift_z(blocks[s - 1, 0])
        for k in range(1, inner):
            if s == outer - 1 and s > 0:
                half = frames // 2
                first = shift_y(blocks[s, 0][:half], k)
                second = shift_z(blocks[s - 1, k][half:])
                blocks[s, k] = jnp.concatenate([first, second], axis=0)
            else:
                blocks[s, k] = shift_y(blocks[s, 0], k)

    def onehot_of(owner_core):
        ids = jnp.concatenate(
            [
                ((x + k) % across * cores + owner_core) * owned
                + jnp.arange(owned, dtype=jnp.int32)
                for k in range(across)
            ]
        )
        return (cycle_map[None, :] == ids[:, None]).astype(jnp.bfloat16)

    mine = onehot_of(core)
    theirs = onehot_of((core + 1) % cores)
    extended = jnp.concatenate([intensity, jnp.ones((8, pixels), jnp.bfloat16)], axis=0)
    rows = frames + 8

    def gram(onehot, right):
        masked = (onehot[:, None, :] * extended[None, :, :]).reshape(-1, pixels)
        return lax.dot_general(
            masked, right, (((1,), (1,)), ((), ())), preferred_element_type=jnp.float32
        ).reshape(onehot.shape[0], rows, right.shape[0])

    low, high = math.log2(0.0218), math.log2(6800.0 * pixels * cores)
    centre, steps = (high + low) / 2, 65400 / (high - low)
    zero = -32700 + 32

    def reduce_owned(g, right):
        if cores > 1:
            away = gram(theirs, right)
            away = swap_core(away)
        here = gram(mine, right)
        if cores > 1:
            here = here + away
        total = here[:owned]
        for k in range(1, across):
            sent = here[k * owned : (k + 1) * owned]
            if g > 0:
                level = (jnp.log2(jnp.maximum(sent, 0.0218)) - centre) * steps
                sent = jnp.round(level).astype(jnp.int16)
            got = shift_x(sent, k)
            if g > 0:
                level = got.astype(jnp.float32)
                got = jnp.where(level > zero, jnp.exp2(level * (1.0 / steps) + centre), 0.0)
            total = total + got
        return total

    groups = [[(0, 0)]]
    for s in range(outer):
        later = [(s, k) for k in range(1, inner)]
        if s + 1 < outer:
            later.append((s + 1, 0))
        if later:
            groups.append(later)

    out = jnp.zeros((owned, frames, tm * frames), jnp.float32)
    for g, members in enumerate(groups):
        if g == 0:
            total = reduce_owned(0, extended)
            row_sums = total[:, :frames, frames]
            scale = total[:, frames, frames][:, None, None] / row_sums[:, :, None]
        else:
            total = reduce_owned(g, jnp.concatenate([blocks[at] for at in members], axis=0))
        for i, (s, k) in enumerate(members):
            part = total[:, :, i * frames : (i + 1) * frames]
            value = part[:, :frames] * scale / part[:, frames : frames + 1]
            at = ((z - s) % outer * inner + (y - k) % inner) * frames
            out = lax.dynamic_update_slice_in_dim(out, value, at, 2)
    return out


def solution(mesh):
    placed = (P("tm", "pix"), P("pix"), P("pix"), P("pix"))

    return jax.shard_map(
        per_device, mesh=mesh, in_specs=placed, out_specs=P("pix", "tm", None), check_vma=False
    )
```
